256 devices in a mesh: ctx: 64 (over x, z_lo, y, core), head: 4 (over z_hi).
Axes of the slice: x: 4, y: 4, z: 8 (z_hi: 4, z_lo: 2; z = z_hi * 2 + z_lo), core: 2. Of those that a mesh axis runs over, the one named last changes fastest.
Arguments:
- query_vecs: bfloat16 [16384, 4096], P('ctx', 'head'), may hold values from -16 to 16
- key_vecs: bfloat16 [16384, 4096], P('ctx', 'head'), may hold values from -16 to 16
- value_vecs: bfloat16 [16384, 4096], P('ctx', 'head'), may hold values from -9 to 9
- out_grad: bfloat16 [16384, 4096], P('ctx', 'head'), may hold values from -9 to 9
- block_mask: int32 [256, 4], P('ctx'), may hold values from -1 to 255, as said below
- norm_gain: float32 [32, 128], P('head'), may hold values from 0.25 to 1.75
Outputs:
- normed: bfloat16 [16384, 4096], P('ctx', 'head')
- query_grad: bfloat16 [16384, 4096], P('ctx', 'head')
- key_grad: bfloat16 [16384, 4096], P('ctx', 'head')
- value_grad: bfloat16 [16384, 4096], P('ctx', 'head')
- gain_grad: float32 [32, 128], P('head')
The draws below stay inside these ranges and needn't reach their ends.
Inputs may be any that keep to these rules, and one draw needn't show every extreme that they name: `block_mask`: entry 0 of row b is b; every other entry is -1 (no block) or a block index within 2 of b, and the indices of one row are distinct.
All inputs are finite; a program needn't handle non-finite values.
Results may differ from the reference program's by a relative error of at most 0.0073.
Values may be sent and summed in bfloat16 or wider, within the bound.
No kernel may reach another device: no remote copies, remote signals or barrier semaphores. Data moves between devices by JAX's collectives and lax.ppermute only.
A program may use at most 128 MiB of HBM per device.

```python
import math
import jax
import jax.numpy as jnp
from jax import lax

HEADS = 32
HEAD_FEATURES = 128
BLOCK = 64
BAND = 2
SLOTS = 4
WIDTH = 4096
SEQUENCE_LENGTH = 16384
NBLOCKS = 256


def pair_draw(key):
    inner_key = jax.random.fold_in(key, 11)
    key_first, key_second = jax.random.split(inner_key, 2)
    dims_all = (SEQUENCE_LENGTH, WIDTH)
    query_part = jax.random.truncated_normal(key_first, -6.0, 6.0, dims_all, jnp.float32)
    key_part = jax.random.truncated_normal(key_second, -6.0, 6.0, dims_all, jnp.float32)
    return (query_part, key_part)


def draw_query_vecs(key, part):
    return pair_draw(key)[0].astype(jnp.bfloat16)


def draw_key_vecs(key, part):
    return pair_draw(key)[1].astype(jnp.bfloat16)


def draw_value_vecs(key, part):
    inner_key = jax.random.fold_in(key, 23)
    dims_all = (SEQUENCE_LENGTH, WIDTH)
    head_of = (jnp.arange(WIDTH) // HEAD_FEATURES).astype(jnp.float32) / (HEADS - 1)
    factor = 0.5 + head_of
    values_raw = jax.random.truncated_normal(inner_key, -6.0, 6.0, dims_all, jnp.float32)
    return (values_raw * factor[None, :]).astype(jnp.bfloat16)


def draw_out_grad(key, part):
    inner_key = jax.random.fold_in(key, 37)
    key_first = jax.random.fold_in(inner_key, 0)
    dims_all = (SEQUENCE_LENGTH, WIDTH)
    along = jnp.arange(SEQUENCE_LENGTH).astype(jnp.float32) / (SEQUENCE_LENGTH - 1)
    factor = 0.5 + along
    grads_raw = jax.random.truncated_normal(key_first, -6.0, 6.0, dims_all, jnp.float32) * factor[:, None]
    return grads_raw.astype(jnp.bfloat16)


def draw_block_mask(key, part):
    inner_key = jax.random.fold_in(key, 29)
    key_first, key_second = jax.random.split(inner_key)
    row_ids = jnp.arange(NBLOCKS)
    logit_scores = jax.random.randint(key_first, (NBLOCKS, 2 * BAND), 0, 1048576) * (2 * BAND) + jnp.arange(2 * BAND)[None, :]
    ranked = jnp.argsort(logit_scores, axis=1, stable=True)[:, :SLOTS - 1]
    offsets = jnp.where(ranked < BAND, ranked - BAND, ranked - BAND + 1)
    target = row_ids[:, None] + offsets
    retained = jax.random.randint(key_second, (NBLOCKS, SLOTS - 1), 0, 4) != 0
    retained = retained & (target >= 0) & (target < NBLOCKS)
    retained = retained.at[0, SLOTS - 2].set(False)
    listed = jnp.where(retained, target, -1)
    return jnp.concatenate([row_ids[:, None], listed], axis=1).astype(jnp.int32)


def setup_inputs(seed: int = 0) -> dict:
    key_list = jax.random.split(jax.random.key(seed), 7)
    return {
        "query_vecs": draw_query_vecs(jax.random.fold_in(key_list[6], 71), 0),
        "key_vecs": draw_key_vecs(jax.random.fold_in(key_list[6], 71), 0),
        "value_vecs": draw_value_vecs(jax.random.fold_in(key_list[6], 71), 0),
        "out_grad": draw_out_grad(jax.random.fold_in(key_list[6], 71), 0),
        "block_mask": draw_block_mask(jax.random.fold_in(key_list[6], 71), 0),
        "norm_gain": jnp.clip(1.0 + 0.15 * jax.random.normal(key_list[5], (HEADS, HEAD_FEATURES), jnp.float32), 0.25, 1.75),
    }


def flip_strand(field_in):
    shaped = field_in.reshape(SEQUENCE_LENGTH, HEADS, HEAD_FEATURES)
    return shaped[::-1, ::-1, :].reshape(SEQUENCE_LENGTH, WIDTH)

def split_heads(field_in):
    return jnp.transpose(field_in.reshape(SEQUENCE_LENGTH, HEADS, HEAD_FEATURES), (1, 0, 2))

def join_heads(stacked):
    return jnp.transpose(stacked, (1, 0, 2)).reshape(SEQUENCE_LENGTH, WIDTH)

def listed_blocks(field_in, slot_index):
    picked = field_in.reshape(NBLOCKS, BLOCK, HEAD_FEATURES)[slot_index]
    return picked.reshape(NBLOCKS, SLOTS * BLOCK, HEAD_FEATURES).astype(jnp.float32)

def head_weights(query_head, key_head, block_mask):
    is_live = block_mask >= 0
    slot_index = jnp.where(is_live, block_mask, 0).astype(jnp.int32)
    query_block_list = query_head.reshape(NBLOCKS, BLOCK, HEAD_FEATURES).astype(jnp.float32)
    key_row_vectors = listed_blocks(key_head, slot_index)
    logit_scores = jnp.einsum('xpf,xzf->xpz', query_block_list, key_row_vectors) * HEAD_FEATURES ** (-0.5)
    columns = jnp.repeat(is_live, BLOCK, axis=1)
    logit_scores = jnp.where(columns[:, None, :], logit_scores, -1e+30)
    highest = lax.optimization_barrier(jnp.max(logit_scores, axis=-1, keepdims=True))
    powers = jnp.exp(logit_scores - highest)
    weights = powers / lax.optimization_barrier(jnp.sum(powers, axis=-1, keepdims=True))
    return (weights, slot_index, query_block_list, key_row_vectors)

def strand_forward(query_in, key_in, value_in, block_mask):

    def one_head(operands):
        query_head, key_head, value_head = operands
        weights, slot_index, query_block_list, key_row_vectors = head_weights(query_head, key_head, block_mask)
        rounded_values = lax.optimization_barrier(weights.astype(jnp.bfloat16)).astype(jnp.float32)
        value_row_vectors = listed_blocks(value_head, slot_index)
        return jnp.einsum('xes,xsg->xeg', rounded_values, value_row_vectors).reshape(SEQUENCE_LENGTH, HEAD_FEATURES)
    return join_heads(lax.map(one_head, (split_heads(query_in), split_heads(key_in), split_heads(value_in))))

def strand_backward(query_in, key_in, value_in, grad_in, block_mask):

    def one_head(operands):
        query_head, key_head, value_head, grad_head = operands
        weights, slot_index, query_block_list, key_row_vectors = head_weights(query_head, key_head, block_mask)
        rounded_values = lax.optimization_barrier(weights.astype(jnp.bfloat16)).astype(jnp.float32)
        value_row_vectors = listed_blocks(value_head, slot_index)
        gradient_block_list = grad_head.reshape(NBLOCKS, BLOCK, HEAD_FEATURES).astype(jnp.float32)
        value_contributions = jnp.einsum('xvf,xva->xfa', rounded_values, gradient_block_list)
        weight_gradient = jnp.einsum('xpf,xzf->xpz', gradient_block_list, value_row_vectors)
        centre = lax.optimization_barrier(jnp.sum(weights * weight_gradient, axis=-1, keepdims=True))
        score_gradient = lax.optimization_barrier((weights * (weight_gradient - centre)).astype(jnp.bfloat16)).astype(jnp.float32)
        query_contributions = jnp.einsum('xes,xsg->xeg', score_gradient, key_row_vectors) * HEAD_FEATURES ** (-0.5)
        key_contributions = jnp.einsum('xvf,xva->xfa', score_gradient, query_block_list) * HEAD_FEATURES ** (-0.5)
        flat_index = slot_index.reshape(NBLOCKS * SLOTS)
        key_total = jnp.zeros((NBLOCKS, BLOCK, HEAD_FEATURES), jnp.float32).at[flat_index].add(key_contributions.reshape(NBLOCKS * SLOTS, BLOCK, HEAD_FEATURES))
        value_total = jnp.zeros((NBLOCKS, BLOCK, HEAD_FEATURES), jnp.float32).at[flat_index].add(value_contributions.reshape(NBLOCKS * SLOTS, BLOCK, HEAD_FEATURES))
        return (query_contributions.reshape(SEQUENCE_LENGTH, HEAD_FEATURES), key_total.reshape(SEQUENCE_LENGTH, HEAD_FEATURES), value_total.reshape(SEQUENCE_LENGTH, HEAD_FEATURES))
    query_part, key_part, value_part = lax.map(one_head, (split_heads(query_in), split_heads(key_in), split_heads(value_in), split_heads(grad_in)))
    return (join_heads(query_part), join_heads(key_part), join_heads(value_part))

def reference(query_vecs, key_vecs, value_vecs, out_grad, block_mask, norm_gain):
    flat_gain = norm_gain.reshape(WIDTH)
    forward_part = strand_forward(query_vecs, key_vecs, value_vecs, block_mask)
    query_flip = flip_strand(query_vecs)
    key_flip = flip_strand(key_vecs)
    value_flip = flip_strand(value_vecs)
    reverse_part = flip_strand(strand_forward(query_flip, key_flip, value_flip, block_mask))
    mixed_sum = forward_part + reverse_part
    rms_root = jnp.sqrt(lax.optimization_barrier(jnp.sum(mixed_sum * mixed_sum, axis=1, keepdims=True)) / WIDTH + 1e-06)
    normed = (flat_gain * mixed_sum / rms_root).astype(jnp.bfloat16)
    grad_values = out_grad.astype(jnp.float32)
    scaled_grad = flat_gain * grad_values
    inner_sum = lax.optimization_barrier(jnp.sum(scaled_grad * mixed_sum, axis=1, keepdims=True)) / WIDTH
    mixed_grad = (scaled_grad / rms_root - mixed_sum * inner_sum / (rms_root * rms_root * rms_root)).astype(jnp.bfloat16)
    gain_grad = (lax.optimization_barrier(jnp.sum(grad_values * mixed_sum / rms_root, axis=0)) / math.sqrt(SEQUENCE_LENGTH)).reshape(HEADS, HEAD_FEATURES)
    query_one, key_one, value_one = strand_backward(query_vecs, key_vecs, value_vecs, mixed_grad, block_mask)
    query_two, key_two, value_two = strand_backward(query_flip, key_flip, value_flip, flip_strand(mixed_grad), block_mask)
    query_grad = (query_one + flip_strand(query_two)).astype(jnp.bfloat16)
    key_grad = (key_one + flip_strand(key_two)).astype(jnp.bfloat16)
    value_grad = (value_one + flip_strand(value_two)).astype(jnp.bfloat16)
    return (normed, query_grad, key_grad, value_grad, gain_grad)
```

```python
import functools
import math

import jax
import jax.numpy as jnp
from jax import lax
from jax.experimental import pallas as pl
from jax.experimental.pallas import tpu as pltpu
from jax.sharding import PartitionSpec as P

HEAD_FEATURES = 128
BLOCK = 64
BAND = 2
BLOCKS_DEV = 4
SLOTS = 4
WIDTH = 4096
PAIR = 2 * BLOCK
TILE = 6
FACTOR = HEAD_FEATURES ** (-0.5)
FACTOR2 = FACTOR * math.log2(math.e)
NT = (((1,), (1,)), ((), ()))
NN = (((1,), (0,)), ((), ()))
TN = (((0,), (0,)), ((), ()))
F32 = jnp.float32
BF16 = jnp.bfloat16
VM = pl.BlockSpec(memory_space=pltpu.VMEM)
SM = pl.BlockSpec(memory_space=pltpu.SMEM)


def dot(a, b, dims):
    return lax.dot_general(a, b, dims, preferred_element_type=F32)


def lanes(head):
    return pl.ds(pl.multiple_of(head * HEAD_FEATURES, HEAD_FEATURES), HEAD_FEATURES)


def list_bias(mask_ref, mirror_ref, first, all_blocks):
    result = []
    for strand in range(2):
        rows = []
        for b in range(BLOCKS_DEV):
            row = {}
            for offset in range(-BAND, BAND + 1):
                target = first + b + offset
                hit = None
                for n in range(SLOTS):
                    if strand == 0:
                        entry = mask_ref[b, n]
                        same = (entry >= 0) & (entry == target)
                    else:
                        entry = mirror_ref[BLOCKS_DEV - 1 - b, n]
                        same = (entry >= 0) & (all_blocks - 1 - entry == target)
                    hit = same if hit is None else hit | same
                row[offset] = jnp.where(hit, 0.0, -1e30).astype(F32)
            rows.append(row)
        result.append(rows)
    return result


def pair_bias(bias, strand, pair):
    left = lax.broadcasted_iota(jnp.int32, (1, 1, PAIR), 2) < BLOCK
    rows = []
    for j in range(TILE):
        scalars = []
        for b in range(2):
            offset = j - BAND - b
            inside = -BAND <= offset <= BAND
            scalars.append(bias[strand][2 * pair + b][offset] if inside else -1e30)
        rows.append(jnp.where(left, scalars[0], scalars[1]).astype(F32))
    return jnp.concatenate(rows, axis=0)


def pair_tiles(own, low, high):
    shape = (TILE, BLOCK, PAIR)
    first = jnp.concatenate([low, own[:, :PAIR]], axis=0).reshape(shape)
    second = jnp.concatenate([own[:, PAIR:], high], axis=0).reshape(shape)
    return first, second


def scores(query, key_own, key_low, key_high):
    own = dot(key_own, query, NT)
    low = dot(key_low, query[:PAIR], NT)
    high = dot(key_high, query[PAIR:], NT)
    return pair_tiles(own, low, high)


def forward_kernel(
    mask_ref, mirror_ref, q_ref, k_ref, v_ref, low_ref, high_ref, g_ref, gain_ref,
    mixed_ref, rows_ref, stats_ref, bias_ref, square_ref, inner_ref,
):
    heads = q_ref.shape[1] // HEAD_FEATURES
    devices = lax.axis_size("ctx")
    first = lax.axis_index("ctx") * BLOCKS_DEV
    bias = list_bias(mask_ref, mirror_ref, first, devices * BLOCKS_DEV)
    for strand in range(2):
        for pair in range(2):
            bias_ref[strand, pair] = pair_bias(bias, strand, pair)
    square_ref[...] = jnp.zeros_like(square_ref)
    inner_ref[...] = jnp.zeros_like(inner_ref)

    @pl.loop(0, heads)
    def _(head):
        at = lanes(head)
        query = q_ref[:, at]
        tiles = scores(query, k_ref[:, at], low_ref[0, :, at], high_ref[0, :, at])
        gain = gain_ref[pl.ds(head, 1), :]
        for pair in range(2):
            x = tiles[pair] * FACTOR2
            peak = jnp.max(x, axis=1, keepdims=True)
            p = jnp.exp2(x - peak)
            mass = jnp.sum(p, axis=1, keepdims=True)
            parts = []
            for strand in range(2):
                shifted = peak + bias_ref[strand, pair]
                top = jnp.max(shifted, axis=0, keepdims=True)
                f = jnp.exp2(shifted - top)
                total = jnp.sum(f * mass, axis=0, keepdims=True)
                parts.append(f / total)
            both = parts[0] + parts[1]
            for i, part in enumerate((peak, parts[0], parts[1])):
                rows_ref[head, pair, i] = part[:, 0, :]
            w = (p * both).astype(BF16).reshape(TILE * BLOCK, PAIR)
            if pair == 0:
                v = jnp.concatenate([low_ref[1, :, at], v_ref[:, at]], axis=0)
            else:
                v = jnp.concatenate([v_ref[:, at], high_ref[1, :, at]], axis=0)
            mixed = dot(w, v, TN)
            here = slice(pair * PAIR, (pair + 1) * PAIR)
            mixed_ref[here, at] = mixed
            square_ref[here] += mixed * mixed
            inner_ref[here] += gain * g_ref[here, at].astype(F32) * mixed

    for pair in range(2):
        here = slice(pair * PAIR, (pair + 1) * PAIR)
        for i, ref in enumerate((square_ref, inner_ref)):
            stats_ref[i : i + 1, here] = jnp.sum(ref[here].T, axis=0, keepdims=True)


def backward_kernel(
    stats_ref, q_ref, k_ref, v_ref, low_ref, high_ref, g_ref, gain_ref, mixed_ref, rows_ref,
    normed_ref, dq_ref, own_ref, to_low_ref, to_high_ref, gain_part_ref, one_ref, two_ref,
):
    heads = q_ref.shape[1] // HEAD_FEATURES
    stats = jnp.sum(stats_ref[...], axis=0)
    root = jnp.sqrt(stats[0:1] / WIDTH + 1e-06)
    inverse = 1.0 / root
    slope = (stats[1:2] / WIDTH) * inverse * inverse * inverse
    for pair in range(2):
        here = slice(pair * PAIR, (pair + 1) * PAIR)
        one_ref[here] = jnp.broadcast_to(inverse[:, here], (PAIR, PAIR)).T
        two_ref[here] = jnp.broadcast_to(slope[:, here], (PAIR, PAIR)).T

    @pl.loop(0, heads)
    def _(head):
        at = lanes(head)
        gain = gain_ref[pl.ds(head, 1), :]
        mixed = mixed_ref[:, at]
        raw = g_ref[:, at].astype(F32)
        unit = mixed * one_ref[...]
        normed_ref[:, at] = (gain * unit).astype(BF16)
        gain_part_ref[pl.ds(head, 1), :] = jnp.sum(raw * unit, axis=0, keepdims=True)
        grad = (gain * raw * one_ref[...] - mixed * two_ref[...]).astype(BF16)
        query = q_ref[:, at]
        key = k_ref[:, at]
        tiles = scores(query, key, low_ref[0, :, at], high_ref[0, :, at])
        slopes = scores(grad, v_ref[:, at], low_ref[1, :, at], high_ref[1, :, at])
        ws, ds = [], []
        for pair in range(2):
            peak, f0, f1 = (rows_ref[head, pair, i][:, None, :] for i in range(3))
            p = jnp.exp2(tiles[pair] * FACTOR2 - peak)
            both = f0 + f1
            slope = slopes[pair]
            mass = jnp.sum(p * slope, axis=1, keepdims=True)
            c0 = jnp.sum(f0 * mass, axis=0, keepdims=True)
            c1 = jnp.sum(f1 * mass, axis=0, keepdims=True)
            shape = (TILE * BLOCK, PAIR)
            ws.append((p * both).astype(BF16).reshape(shape))
            ds.append((p * (both * slope - (f0 * c0 + f1 * c1))).astype(BF16).reshape(shape))
        w_own = jnp.concatenate([ws[0][PAIR:], ws[1][: 2 * PAIR]], axis=1)
        d_own = jnp.concatenate([ds[0][PAIR:], ds[1][: 2 * PAIR]], axis=1)
        own_ref[0, :, at] = dot(d_own, query, NN) * FACTOR
        own_ref[1, :, at] = dot(w_own, grad, NN)
        to_low_ref[0, :, at] = (dot(ds[0][:PAIR], query[:PAIR], NN) * FACTOR).astype(BF16)
        to_low_ref[1, :, at] = dot(ws[0][:PAIR], grad[:PAIR], NN).astype(BF16)
        to_high_ref[0, :, at] = (dot(ds[1][2 * PAIR :], query[PAIR:], NN) * FACTOR).astype(BF16)
        to_high_ref[1, :, at] = dot(ws[1][2 * PAIR :], grad[PAIR:], NN).astype(BF16)
        dq = dot(d_own, key, TN)
        dq_low = dot(ds[0][:PAIR], low_ref[0, :, at], TN)
        dq_high = dot(ds[1][2 * PAIR :], high_ref[0, :, at], TN)
        dq_ref[:PAIR, at] = ((dq[:PAIR] + dq_low) * FACTOR).astype(BF16)
        dq_ref[PAIR:, at] = ((dq[PAIR:] + dq_high) * FACTOR).astype(BF16)


def settle_kernel(own_ref, from_low_ref, from_high_ref, dk_ref, dv_ref):
    for i, out in enumerate((dk_ref, dv_ref)):
        out[:PAIR] = (own_ref[i, :PAIR] + from_low_ref[i].astype(F32)).astype(BF16)
        out[PAIR:] = (own_ref[i, PAIR:] + from_high_ref[i].astype(F32)).astype(BF16)


def shifted(shard, by):
    devices = lax.axis_size("ctx")
    pairs = [(i, i + by) for i in range(devices) if 0 <= i + by < devices]
    return lax.ppermute(shard, "ctx", pairs)


def copy_for_each(shard, axis):
    devices = lax.axis_size(axis)
    return lax.all_to_all(
        jnp.broadcast_to(shard[None], (devices, *shard.shape)), axis, 0, 0, tiled=True
    )


def shape(dims, dtype):
    return jax.ShapeDtypeStruct(dims, dtype)


def body(query_vecs, key_vecs, value_vecs, out_grad, block_mask, norm_gain):
    own_rows, features = query_vecs.shape
    heads = features // HEAD_FEATURES
    devices = lax.axis_size("ctx")
    to_next = jnp.stack([key_vecs[PAIR:], value_vecs[PAIR:]])
    to_previous = jnp.stack([key_vecs[:PAIR], value_vecs[:PAIR]])
    low = shifted(to_next, 1)
    high = shifted(to_previous, -1)
    mirror = lax.ppermute(block_mask, "ctx", [(i, devices - 1 - i) for i in range(devices)])
    mixed, rows, stats = pl.pallas_call(
        forward_kernel,
        out_shape=(
            shape((own_rows, features), F32),
            shape((heads, 2, 3, TILE, PAIR), F32),
            shape((2, own_rows), F32),
        ),
        in_specs=[SM, SM] + [VM] * 7,
        out_specs=(VM, VM, VM),
        scratch_shapes=[
            pltpu.VMEM((2, 2, TILE, 1, PAIR), F32),
            pltpu.VMEM((own_rows, HEAD_FEATURES), F32),
            pltpu.VMEM((own_rows, HEAD_FEATURES), F32),
        ],
        name="forward",
    )(block_mask, mirror, query_vecs, key_vecs, value_vecs, low, high, out_grad, norm_gain)
    all_stats = copy_for_each(stats, "head")
    normed, query_grad, own, to_low, to_high, gain_part = pl.pallas_call(
        backward_kernel,
        out_shape=(
            shape((own_rows, features), BF16),
            shape((own_rows, features), BF16),
            shape((2, own_rows, features), F32),
            shape((2, PAIR, features), BF16),
            shape((2, PAIR, features), BF16),
            shape((heads, HEAD_FEATURES), F32),
        ),
        in_specs=[VM] * 10,
        out_specs=(VM,) * 6,
        scratch_shapes=[pltpu.VMEM((own_rows, HEAD_FEATURES), F32)] * 2,
        name="backward",
    )(
        all_stats, query_vecs, key_vecs, value_vecs, low, high, out_grad, norm_gain, mixed, rows
    )
    from_high = shifted(to_low, -1)
    from_low = shifted(to_high, 1)
    gain_grad = copy_for_each(gain_part, "ctx").sum(axis=0) / math.sqrt(own_rows * devices)
    key_grad, value_grad = pl.pallas_call(
        settle_kernel,
        out_shape=(shape((own_rows, features), BF16),) * 2,
        in_specs=[VM] * 3,
        out_specs=(VM,) * 2,
        name="settle",
    )(own, from_low, from_high)
    return (normed, query_grad, key_grad, value_grad, gain_grad)


def solution(mesh):
    return jax.shard_map(
        body,
        mesh=mesh,
        in_specs=(
            P("ctx", "head"),
            P("ctx", "head"),
            P("ctx", "head"),
            P("ctx", "head"),
            P("ctx", None),
            P("head", None),
        ),
        out_specs=(
            P("ctx", "head"),
            P("ctx", "head"),
            P("ctx", "head"),
            P("ctx", "head"),
            P("head", None),
        ),
        check_vma=False,
    )
```
